32 devices in a mesh: ctx: 8 (over z, y), head: 4 (over x, core).
Axes of the slice: x: 2, y: 2, z: 4, core: 2. Of those that a mesh axis runs over, the one named last changes fastest.
Arguments:
- q_nope: bfloat16 [2048, 16384], P('ctx', 'head'), may hold values from -4 to 4
- q_rope: bfloat16 [2048, 8192], P('ctx', 'head'), may hold values from -8 to 8
- kv_latent: bfloat16 [2048, 576], P(('ctx', 'head')), may hold values from -6 to 6
- half_order: int32 [16], replicated, may hold values from 0 to 15, as said below
- w_uk: bfloat16 [128, 128, 512], P('head'), may hold values from -0.5 to 0.5
- w_uv: bfloat16 [128, 512, 128], P('head'), may hold values from -1.5 to 1.5
Outputs:
- attended: bfloat16 [2048, 16384], P('ctx', 'head')
The draws below stay inside these ranges and needn't reach their ends.
Inputs may be any that keep to these rules, and one draw needn't show every extreme that they name: `half_order`: a permutation of 0 to 15.
All inputs are finite; a program needn't handle non-finite values.
Results may differ from the reference program's by a relative error of at most 0.0085.
Values may be sent and summed in bfloat16 or wider, within the bound.
A program may use at most 128 MiB of HBM per device.

```python
import jax
import jax.numpy as jnp
from jax import lax

HEADS = 128
LATENT = 512
ROPE = 64
NOPE = 128
VDIM = 128
TOKENS = 2048
HALVES = 16


def order_of(key):
    return jax.random.permutation(jax.random.fold_in(key, 11), HALVES).astype(jnp.int32)


def draw_half_order(key, part):
    return order_of(key)


def draw_q_rope(key, part):
    inner_key = jax.random.fold_in(key, 31)
    base = jnp.clip(jax.random.normal(inner_key, (TOKENS, HEADS, ROPE), jnp.float32), -4.0, 4.0)
    return base.reshape(TOKENS, HEADS * ROPE).astype(jnp.bfloat16)


def draw_kv_latent(key, part):
    inner_key = jax.random.fold_in(key, 41)
    base = jnp.clip(jax.random.normal(inner_key, (TOKENS, LATENT + ROPE), jnp.float32), -4.0, 4.0)
    return base.astype(jnp.bfloat16)


def levels(own_key, extent, shards, smallest, top_value):
    def one(dim, parts):
        draws = jax.random.uniform(jax.random.fold_in(jax.random.fold_in(own_key, 6), dim), (parts,), jnp.float32, smallest / len(shards), top_value / len(shards))
        return jnp.repeat(jnp.exp(draws), extent[dim] // parts).reshape((-1,) + (1,) * (len(extent) - dim - 1))

    loudness = one(*shards[0])
    for cut in shards[1:]:
        loudness = loudness * one(*cut)
    return loudness


def noise(rng, dims, deviation, most, cuts=(), kind=jnp.bfloat16):
    drawn = deviation * jax.random.normal(rng, dims, jnp.float32)
    if cuts:
        drawn = drawn * levels(rng, dims, cuts, -0.22, 0.18)
    return jnp.clip(drawn, -most, most).astype(kind)


def setup_inputs(seed: int = 0) -> dict:
    arg_keys = jax.random.split(jax.random.key(seed), 7)
    return {
        "q_nope": noise(arg_keys[0], (TOKENS, HEADS * NOPE), 1.0, 4.0, ((0, 8), (1, 4))),
        "q_rope": draw_q_rope(jax.random.fold_in(arg_keys[6], 71), 0),
        "kv_latent": draw_kv_latent(jax.random.fold_in(arg_keys[6], 71), 0),
        "half_order": draw_half_order(jax.random.fold_in(arg_keys[6], 71), 0),
        "w_uk": noise(arg_keys[4], (HEADS, NOPE, LATENT), NOPE ** -0.5, 0.5, ((0, 4),)),
        "w_uv": noise(arg_keys[5], (HEADS, LATENT, VDIM), (LATENT // 32) ** -0.5, 1.5, ((0, 4),)),
    }


def reference(q_nope, q_rope, kv_latent, half_order, w_uk, w_uv):
    head_count, nope_width, latent_width = w_uk.shape
    value_width = w_uv.shape[2]
    token_count = q_nope.shape[0]
    rope_width = q_rope.shape[1] // head_count
    half_rows = token_count // half_order.shape[0]
    index_rows = jnp.arange(token_count, dtype=jnp.int32)
    position = half_order[index_rows // half_rows] * half_rows + index_rows % half_rows
    visible = position[None, :] <= position[:, None]
    key_latent = kv_latent[:, :latent_width].astype(jnp.float32)
    key_rope = kv_latent[:, latent_width:].astype(jnp.float32)
    score_scale = (nope_width + rope_width) ** -0.5
    queries = q_nope.reshape(token_count, head_count, nope_width).transpose(1, 0, 2)
    query_rope = q_rope.reshape(token_count, head_count, rope_width).transpose(1, 0, 2)

    def one_head(operands):
        query_head, rope_head, key_weight, value_weight = operands
        query_latent = jnp.dot(query_head.astype(jnp.float32), key_weight.astype(jnp.float32)).astype(jnp.bfloat16)
        scores = jnp.dot(query_latent.astype(jnp.float32), key_latent.T) + jnp.dot(rope_head.astype(jnp.float32), key_rope.T)
        scores = scores * score_scale
        masked = jnp.where(visible, scores, -1e30)
        row_max = jnp.max(masked, axis=1, keepdims=True)
        weights = jnp.where(visible, jnp.exp(jnp.minimum(scores - row_max, 0.0)), 0.0)
        weight_sum = jnp.sum(weights, axis=1, keepdims=True)
        summed = jnp.dot(weights.astype(jnp.bfloat16).astype(jnp.float32), key_latent)
        out_latent = (summed / weight_sum).astype(jnp.bfloat16)
        return jnp.dot(out_latent.astype(jnp.float32), value_weight.astype(jnp.float32)).astype(jnp.bfloat16)

    outputs = lax.map(one_head, (queries, query_rope, w_uk, w_uv))
    return outputs.transpose(1, 0, 2).reshape(token_count, head_count * value_width)
```

```python
import functools
import math

import jax
import jax.numpy as jnp
from jax import lax
from jax.experimental import pallas as pl
from jax.experimental.pallas import tpu as pltpu
from jax.sharding import PartitionSpec as P

LANES = 128
HIDDEN = -1e30


def flipped(index, bit):
    return index + bit * (1 - 2 * ((index // bit) % 2))


def hop_orders(ctx_size, head_size, pieces):
    base = [("ctx", 1 << k) for k in reversed(range(ctx_size.bit_length() - 1))]
    base += [("head", 1 << k) for k in reversed(range(1, head_size.bit_length() - 1))]
    if len(base) < 4:
        return [base] * pieces
    orders = [
        base,
        base[:-2] + [base[-1], base[-2]],
        [base[-2], base[0], base[-1]] + base[1:-2],
        [base[0], base[-1]] + base[1:-2] + [base[-2]],
    ]
    return [orders[piece % 4] for piece in range(pieces)]


def slot_mask(order, slot, head_size):
    hops = order + [("head", 1)]
    taken = [hop for k, hop in enumerate(hops) if (slot >> k) & 1]
    return sum(bit * (head_size if axis == "ctx" else 1) for axis, bit in taken)


def chunk_plan(hops, pieces, piece_rows, limit):
    other = 1 << hops
    level = 0
    while level < hops and 2 * pieces * piece_rows << (level + 1) <= limit:
        level += 1
    first = [(piece, side, 1 << level) for side in (0, other) for piece in range(pieces)]
    chunks = [(level, level, first)]
    for k in range(level + 1, hops + 1):
        start, size = 1 << (k - 1), 1 << (k - 1)
        own = [(piece, start, size) for piece in range(pieces)]
        far = [(piece, other + start, size) for piece in range(pieces)]
        side_rows = pieces * size * piece_rows
        if 2 * side_rows <= limit:
            chunks.append((k, k, own + far))
            continue
        for side, runs in ((False, own), (True, far)):
            parts = -(-side_rows // limit)
            for part in range(parts):
                cut = size // parts
                chunks.append((k, k if side else -1, [(piece, run + part * cut, cut) for piece, run, _ in runs]))
    return chunks


def fused_kernel(
    scale,
    orders,
    head_size,
    chunks,
    comm,
    half_pos,
    q_nope_hbm,
    q_rope_hbm,
    kv_hbm,
    w_uk_hbm,
    w_uv_hbm,
    out_ref,
    kv_all,
    q_main,
    q_side,
    rope_in,
    w_uk,
    w_uv_in,
    w_uv,
    q_pos,
    keys,
    key_side_even,
    key_side_odd,
    values_even,
    values_odd,
    s_even_0,
    s_even_1,
    s_odd_0,
    s_odd_1,
    peaks,
    peak_all,
    den_all,
    acc_all,
    own_sem,
    in_sem,
    send_sem,
    recv_sem,
    core_send_sem,
    core_recv_sem,
):
    place = {"ctx": lax.axis_index("ctx"), "head": lax.axis_index("head")}
    device = place["ctx"] * head_size + place["head"]
    pieces, slots, piece_rows, _ = kv_all.shape
    hops = len(orders[0])
    heads, queries, nope_width = q_main.shape
    pairs = heads // 2
    latent_width = w_uk.shape[2]
    value_width = w_uv.shape[1]
    rope_width = kv_all.shape[3] - latent_width
    rows = pieces * piece_rows
    half_rows = rows * slots // half_pos.shape[0]
    halves = queries // half_rows
    sources = half_rows // rows

    def partner(axis, bit):
        return {**place, axis: flipped(place[axis], bit)}

    own = []
    for piece in range(pieces):
        own.append(
            pltpu.make_async_copy(
                kv_hbm.at[pl.ds(piece * piece_rows, piece_rows), :], kv_all.at[piece, 0], own_sem.at[piece]
            )
        )
        own[-1].start()
    loads = [
        pltpu.make_async_copy(w_uv_hbm, w_uv_in, in_sem.at[0]),
        pltpu.make_async_copy(w_uk_hbm, w_uk, in_sem.at[1]),
    ]
    for head in range(heads):
        loads.append(
            pltpu.make_async_copy(
                q_nope_hbm.at[:, pl.ds(head * nope_width, nope_width)], q_main.at[head], in_sem.at[2 + head]
            )
        )
    for pair in range(pairs):
        loads.append(
            pltpu.make_async_copy(
                q_rope_hbm.at[:, pl.ds(pair * LANES, LANES)], rope_in.at[pair], in_sem.at[2 + heads + pair]
            )
        )
    for load in loads:
        load.start()

    def hop(piece, k):
        size = 1 << k
        return pltpu.make_async_remote_copy(
            src_ref=kv_all.at[piece, pl.ds(0, size)],
            dst_ref=kv_all.at[piece, pl.ds(size, size)],
            send_sem=send_sem.at[piece, k],
            recv_sem=recv_sem.at[piece, k],
            device_id=partner(*orders[piece][k]),
            device_id_type=pl.DeviceIdType.MESH,
        )

    def across(piece, k):
        start, size = (0, 1) if k == 0 else (1 << (k - 1), 1 << (k - 1))
        return pltpu.make_async_remote_copy(
            src_ref=kv_all.at[piece, pl.ds(start, size)],
            dst_ref=kv_all.at[piece, pl.ds(slots // 2 + start, size)],
            send_sem=core_send_sem.at[piece, k],
            recv_sem=core_recv_sem.at[piece, k],
            device_id=partner("head", 1),
            device_id_type=pl.DeviceIdType.MESH,
        )

    def advance(k):
        for piece in range(pieces):
            if k == 0:
                own[piece].wait()
            elif comm:
                hop(piece, k - 1).wait_recv()
            if comm:
                if k < hops:
                    hop(piece, k).start()
                across(piece, k).start()

    def crossed(k):
        if comm:
            for piece in range(pieces):
                across(piece, k).wait_recv()

    if comm:
        barrier = pltpu.get_barrier_semaphore()
        greeted = sorted(orders[0]) + [("head", 1)]
        for axis, bit in greeted:
            pl.semaphore_signal(barrier, inc=1, device_id=partner(axis, bit), device_id_type=pl.DeviceIdType.MESH)
        pl.semaphore_wait(barrier, len(greeted))

    def turn_values(first, last):
        @pl.loop(first, last)
        def _(head):
            w_uv[head] = w_uv_in[head].T

    def side_queries(first, last):
        @pl.loop(first, last)
        def _(pair):
            lane = lax.broadcasted_iota(jnp.int32, (queries, LANES), 1)
            half = lax.broadcasted_iota(jnp.int32, (queries, LANES), 0) // half_rows
            rope = rope_in[pair].astype(jnp.float32)
            for odd in range(2):
                base = rope_width * (1 - odd)
                mine = (lane < rope_width) if odd == 0 else (lane >= rope_width)
                flag = jnp.where(lane - base == half, 1.0, 0.0)
                q_side[2 * pair + odd] = jnp.where(mine, rope, flag).astype(jnp.bfloat16)

    advance(0)
    for load in loads[:1]:
        load.wait()
    turn_values(0, heads // 2)
    for k in range(1, chunks[0][0] + 1):
        advance(k)
        if k == 1:
            turn_values(heads // 2, heads)
    for load in loads[1:]:
        load.wait()
    side_queries(0, pairs)
    half_at = [half_pos[place["ctx"] * halves + half] for half in range(halves)]
    for half in range(halves):
        q_pos[:, half * half_rows : (half + 1) * half_rows] = half_at[half] * half_rows + lax.broadcasted_iota(
            jnp.int32, (piece_rows, half_rows), 1
        )
    for k in range(chunks[0][1] + 1):
        crossed(k)
    level, far_level = chunks[0][:2]

    def compute(index, middle):
        _, _, runs = chunks[index]
        first, last = index == 0, index == len(chunks) - 1
        groups = [(piece, slot) for piece, start, count in runs for slot in range(start, start + count)]
        size = len(groups) * piece_rows
        row = 0
        for piece, start, count in runs:
            end = row + count * piece_rows
            block = kv_all[piece, start : start + count].reshape(count * piece_rows, latent_width + rope_width)
            keys[row:end, :] = block[:, :latent_width]
            key_side_even[row:end, :rope_width] = block[:, latent_width:]
            key_side_odd[row:end, rope_width:] = block[:, latent_width:]
            row = end
        flag_lane = lax.broadcasted_iota(jnp.int32, (piece_rows, LANES - rope_width), 1)
        starts = []
        for g, (piece, slot) in enumerate(groups):
            mask = slot_mask(orders[piece], slot, head_size)
            source = sum(
                lax.rem(lax.div(device, bit), 2) * bit if not mask & bit else (1 - lax.rem(lax.div(device, bit), 2)) * bit
                for bit in [1 << b for b in range((slots - 1).bit_length())]
            )
            block = lax.div(source, sources)
            at = half_pos[block]
            flag = jnp.zeros(flag_lane.shape, jnp.float32)
            for half in range(halves):
                flag = jnp.where(flag_lane == half, jnp.where(at <= half_at[half], 0.0, HIDDEN), flag)
            flag = flag.astype(jnp.bfloat16)
            key_side_even[g * piece_rows : (g + 1) * piece_rows, rope_width:] = flag
            key_side_odd[g * piece_rows : (g + 1) * piece_rows, :rope_width] = flag
            starts.append(
                at * half_rows + (source - block * sources) * rows + piece * piece_rows if mask < head_size else None
            )

        def front(pair, values, scores, slot):
            part = keys[:size, :]
            grown = lax.dot_general(
                part,
                w_uk[pl.ds(2 * pair, 2)].reshape(2 * nope_width, latent_width),
                (((1,), (1,)), ((), ())),
                preferred_element_type=jnp.float32,
            ).astype(jnp.bfloat16)
            values[:, :size] = lax.dot_general(
                w_uv[pl.ds(2 * pair, 2)].reshape(2 * value_width, latent_width),
                part,
                (((1,), (1,)), ((), ())),
                preferred_element_type=jnp.float32,
            ).astype(jnp.bfloat16)
            for odd, side in ((0, key_side_even), (1, key_side_odd)):
                full = jnp.concatenate(
                    [grown[:, odd * nope_width : (odd + 1) * nope_width], side[:size, :]], axis=1
                )
                query = jnp.concatenate([q_main[2 * pair + odd], q_side[2 * pair + odd]], axis=1)
                s = lax.dot_general(full, query, (((1,), (1,)), ((), ())), preferred_element_type=jnp.float32)
                peak = None
                g = 0
                while g < len(groups):
                    h = g + 1
                    if starts[g] is None:
                        while h < len(groups) and starts[h] is None:
                            h += 1
                    piece_s = s[g * piece_rows : h * piece_rows]
                    if starts[g] is not None:
                        key_pos = starts[g] + lax.broadcasted_iota(jnp.int32, piece_s.shape, 0)
                        piece_s = jnp.where(key_pos <= q_pos[...], piece_s, HIDDEN)
                    scores[odd][g * piece_rows : h * piece_rows, :] = piece_s
                    top = jnp.max(piece_s.reshape(-1, 8, queries), axis=0)
                    peak = top if peak is None else jnp.maximum(peak, top)
                    g = h
                peaks[slot * 2 + odd] = peak

        def back(pair, values, scores, slot):
            for odd in range(2):
                head = 2 * pair + odd
                top = jnp.broadcast_to(jnp.max(peaks[slot * 2 + odd], axis=0, keepdims=True), (8, queries))
                if not first:
                    before = peak_all[head]
                    top = jnp.maximum(before, top)
                    fade = jnp.exp2((before - top) * scale)
                if not last:
                    peak_all[head] = top
                weight = jnp.exp2((scores[odd][:size, :].reshape(-1, 8, queries) - top[None]) * scale)
                den = jnp.sum(weight, axis=0)
                total = jnp.dot(
                    values[odd * value_width : (odd + 1) * value_width, :size],
                    weight.reshape(size, queries).astype(jnp.bfloat16),
                    preferred_element_type=jnp.float32,
                )
                if not first:
                    den = den + den_all[head] * fade
                    total = total + (acc_all[head].reshape(-1, 8, queries) * fade[None]).reshape(total.shape)
                if not last:
                    den_all[head] = den
                    acc_all[head] = total
                else:
                    out = total * (1.0 / jnp.sum(den, axis=0, keepdims=True))
                    out_ref[:, pl.ds(pl.multiple_of(head * value_width, value_width), value_width)] = out.T.astype(
                        out_ref.dtype
                    )

        even = (values_even, (s_even_0, s_even_1), 0)
        odd = (values_odd, (s_odd_0, s_odd_1), 1)

        def steps(begin, end):
            @pl.loop(begin, end)
            def _(turn):
                front(2 * turn + 1, *odd)
                back(2 * turn, *even)
                front(2 * turn + 2, *even)
                back(2 * turn + 1, *odd)

        front(0, *even)
        turns = pairs // 2 - 1
        steps(0, turns // 2)
        middle()
        steps(turns // 2, turns)
        front(pairs - 1, *odd)
        back(pairs - 2, *even)
        back(pairs - 1, *odd)

    for index in range(len(chunks)):
        reach = {"level": level}

        def middle(index=index, reach=reach):
            if index + 1 < len(chunks) and chunks[index + 1][0] > level:
                pass

        compute(index, middle)
        if index + 1 < len(chunks):
            needed, far_needed = chunks[index + 1][:2]
            while level < needed:
                level += 1
                advance(level)
            while far_level < far_needed:
                far_level += 1
                crossed(far_level)
    if comm:
        for piece in range(pieces):
            for k in range(hops):
                hop(piece, k).wait_send()
            for k in range(hops + 1):
                across(piece, k).wait_send()


def fused(q_nope, q_rope, kv_latent, half_order, w_uk, w_uv, ctx_size, head_size, comm=True, limit=512):
    heads, nope_width, latent_width = w_uk.shape
    value_width = w_uv.shape[2]
    queries = q_nope.shape[0]
    rope_width = q_rope.shape[1] // heads
    rows, width = kv_latent.shape
    pieces = max(1, min(4, rows // 16))
    orders = hop_orders(ctx_size, head_size, pieces)
    hops = len(orders[0])
    piece_rows = rows // pieces
    slots = ctx_size * head_size
    chunks = chunk_plan(hops, pieces, piece_rows, limit)
    most = max(sum(count for _, _, count in runs) for _, _, runs in chunks) * piece_rows
    scale = (nope_width + rope_width) ** (-0.5) * math.log2(math.e)
    bf16, f32 = jnp.bfloat16, jnp.float32
    dma = pltpu.SemaphoreType.DMA
    scores = pltpu.VMEM((most, queries), f32)
    anywhere = pl.BlockSpec(memory_space=pl.ANY)
    return pl.pallas_call(
        functools.partial(fused_kernel, scale, orders, head_size, chunks, comm),
        out_shape=jax.ShapeDtypeStruct((queries, heads * value_width), bf16),
        in_specs=[pl.BlockSpec(memory_space=pltpu.SMEM)] + [anywhere] * 5,
        out_specs=pl.BlockSpec(memory_space=pltpu.VMEM),
        scratch_shapes=[
            pltpu.VMEM((pieces, slots, piece_rows, width), bf16),
            pltpu.VMEM((heads, queries, nope_width), bf16),
            pltpu.VMEM((heads, queries, LANES), bf16),
            pltpu.VMEM((heads // 2, queries, LANES), bf16),
            pltpu.VMEM((heads, nope_width, latent_width), bf16),
            pltpu.VMEM((heads, latent_width, value_width), bf16),
            pltpu.VMEM((heads, value_width, latent_width), bf16),
            pltpu.VMEM((piece_rows, queries), jnp.int32),
            pltpu.VMEM((most, latent_width), bf16),
            pltpu.VMEM((most, LANES), bf16),
            pltpu.VMEM((most, LANES), bf16),
            pltpu.VMEM((2 * value_width, most), bf16),
            pltpu.VMEM((2 * value_width, most), bf16),
            scores,
            scores,
            scores,
            scores,
            pltpu.VMEM((4, 8, queries), f32),
            pltpu.VMEM((heads, 8, queries), f32),
            pltpu.VMEM((heads, 8, queries), f32),
            pltpu.VMEM((heads, value_width, queries), f32),
            dma((pieces,)),
            dma((2 + heads + heads // 2,)),
            dma((pieces, hops)),
            dma((pieces, hops)),
            dma((pieces, hops + 1)),
            dma((pieces, hops + 1)),
        ],
        compiler_params=pltpu.CompilerParams(
            vmem_limit_bytes=60 * 1024 * 1024,
            **(dict(collective_id=0, has_side_effects=True) if comm else {}),
        ),
        name="attend",
    )(half_order, q_nope, q_rope, kv_latent, w_uk, w_uv)


def on_device(ctx_size, head_size, q_nope, q_rope, kv_latent, half_order, w_uk, w_uv):
    return fused(q_nope, q_rope, kv_latent, half_order, w_uk, w_uv, ctx_size, head_size)


def solution(mesh):
    return jax.shard_map(
        functools.partial(on_device, mesh.shape["ctx"], mesh.shape["head"]),
        mesh=mesh,
        in_specs=(
            P("ctx", "head"),
            P("ctx", "head"),
            P(("ctx", "head"), None),
            P(),
            P("head", None, None),
            P("head", None, None),
        ),
        out_specs=P("ctx", "head"),
        check_vma=False,
    )
```

```python
import functools
import math

import jax
import jax.numpy as jnp
from jax import lax
from jax.experimental import pallas as pl
from jax.experimental.pallas import tpu as pltpu
from jax.sharding import PartitionSpec as P

LANES = 128
HIDDEN = -1e30


def flipped(index, bit):
    return index + bit * (1 - 2 * ((index // bit) % 2))


def hop_orders(ctx_size, head_size, pieces):
    base = [("ctx", 1 << k) for k in reversed(range(ctx_size.bit_length() - 1))]
    base += [("head", 1 << k) for k in reversed(range(1, head_size.bit_length() - 1))]
    if len(base) < 4:
        return [base] * pieces
    orders = [
        base,
        base[:-2] + [base[-1], base[-2]],
        [base[-2], base[0], base[-1]] + base[1:-2],
        [base[0], base[-1]] + base[1:-2] + [base[-2]],
    ]
    return [orders[piece % 4] for piece in range(pieces)]


def slot_mask(order, slot, head_size):
    hops = order + [("head", 1)]
    taken = [hop for k, hop in enumerate(hops) if (slot >> k) & 1]
    return sum(bit * (head_size if axis == "ctx" else 1) for axis, bit in taken)


def chunk_plan(hops, pieces, piece_rows, limit, later):
    other = 1 << hops
    level = 0
    while level < hops and 2 * pieces * piece_rows << (level + 1) <= limit:
        level += 1
    first = [(piece, side, 1 << level) for side in (0, other) for piece in range(pieces)]
    chunks = [(level, level, first)]
    for k in range(level + 1, hops + 1):
        start, size = 1 << (k - 1), 1 << (k - 1)
        own = [(piece, start, size) for piece in range(pieces)]
        far = [(piece, other + start, size) for piece in range(pieces)]
        side_rows = pieces * size * piece_rows
        if 2 * side_rows <= later:
            chunks.append((k, k, own + far))
            continue
        for side, runs in ((False, own), (True, far)):
            parts = -(-side_rows // later)
            for part in range(parts):
                cut = size // parts
                chunks.append((k, k if side else -1, [(piece, run + part * cut, cut) for piece, run, _ in runs]))
    return chunks


BLOCK = 256
WIDE = 2
VMEM_MIB = 48


def order_of_tasks(blocks, wide):
    every = range(blocks)
    plan = []
    for w in range(wide):
        plan += [(w, "b", 0), (w, "b", 1)]
    for w in range(wide):
        for b in every:
            plan += [(w, "k", b), (w, "e", 0, b), (w, "p", 0, b)]
    for w in range(wide):
        for b in every:
            plan += [(w, "v", b), (w, "e", 1, b), (w, "p", 1, b)]
    for w in range(wide):
        for odd in range(2):
            plan += [(w, "s", odd, b) for b in every]
    for w in range(wide):
        plan += [(w, "f", 0), (w, "f", 1)]
    return plan


def fused_kernel(
    scale,
    orders,
    head_size,
    chunks,
    comm,
    wide,
    half_pos,
    q_nope_hbm,
    q_rope_hbm,
    kv_hbm,
    w_uk_hbm,
    w_uv_hbm,
    out_ref,
    kv_all,
    q_main,
    q_side,
    rope_in,
    w_uk,
    w_uv_in,
    w_uv,
    q_pos,
    keys,
    key_side_even,
    key_side_odd,
    values,
    scores,
    peaks,
    peak_all,
    den_all,
    acc_all,
    own_sem,
    in_sem,
    send_sem,
    recv_sem,
    core_send_sem,
    core_recv_sem,
):
    place = {"ctx": lax.axis_index("ctx"), "head": lax.axis_index("head")}
    device = place["ctx"] * head_size + place["head"]
    pieces, slots, piece_rows, _ = kv_all.shape
    hops = len(orders[0])
    heads, queries, nope_width = q_main.shape
    pairs = heads // 2
    latent_width = w_uk.shape[2]
    value_width = w_uv.shape[1]
    rope_width = kv_all.shape[3] - latent_width
    rows = pieces * piece_rows
    half_rows = rows * slots // half_pos.shape[0]
    halves = queries // half_rows
    sources = half_rows // rows

    def partner(axis, bit):
        return {**place, axis: flipped(place[axis], bit)}

    own = []
    for piece in range(pieces):
        own.append(
            pltpu.make_async_copy(
                kv_hbm.at[pl.ds(piece * piece_rows, piece_rows), :], kv_all.at[piece, 0], own_sem.at[piece]
            )
        )
        own[-1].start()
    loads = [
        pltpu.make_async_copy(w_uv_hbm, w_uv_in, in_sem.at[0]),
        pltpu.make_async_copy(w_uk_hbm, w_uk, in_sem.at[1]),
    ]
    for head in range(heads):
        loads.append(
            pltpu.make_async_copy(
                q_nope_hbm.at[:, pl.ds(head * nope_width, nope_width)], q_main.at[head], in_sem.at[2 + head]
            )
        )
    for pair in range(pairs):
        loads.append(
            pltpu.make_async_copy(
                q_rope_hbm.at[:, pl.ds(pair * LANES, LANES)], rope_in.at[pair], in_sem.at[2 + heads + pair]
            )
        )
    for load in loads:
        load.start()

    def hop(piece, k):
        size = 1 << k
        return pltpu.make_async_remote_copy(
            src_ref=kv_all.at[piece, pl.ds(0, size)],
            dst_ref=kv_all.at[piece, pl.ds(size, size)],
            send_sem=send_sem.at[piece, k],
            recv_sem=recv_sem.at[piece, k],
            device_id=partner(*orders[piece][k]),
            device_id_type=pl.DeviceIdType.MESH,
        )

    def across(piece, k):
        start, size = (0, 1) if k == 0 else (1 << (k - 1), 1 << (k - 1))
        return pltpu.make_async_remote_copy(
            src_ref=kv_all.at[piece, pl.ds(start, size)],
            dst_ref=kv_all.at[piece, pl.ds(slots // 2 + start, size)],
            send_sem=core_send_sem.at[piece, k],
            recv_sem=core_recv_sem.at[piece, k],
            device_id=partner("head", 1),
            device_id_type=pl.DeviceIdType.MESH,
        )

    def advance(k):
        for piece in range(pieces):
            if k == 0:
                own[piece].wait()
            elif comm:
                hop(piece, k - 1).wait_recv()
            if comm:
                if k < hops:
                    hop(piece, k).start()
                across(piece, k).start()

    def crossed(k):
        if comm:
            for piece in range(pieces):
                across(piece, k).wait_recv()

    if comm:
        barrier = pltpu.get_barrier_semaphore()
        greeted = sorted(orders[0]) + [("head", 1)]
        for axis, bit in greeted:
            pl.semaphore_signal(barrier, inc=1, device_id=partner(axis, bit), device_id_type=pl.DeviceIdType.MESH)
        pl.semaphore_wait(barrier, len(greeted))

    def turn_values(first, last):
        @pl.loop(first, last)
        def _(head):
            w_uv[head] = w_uv_in[head].T

    def side_queries(first, last):
        @pl.loop(first, last)
        def _(pair):
            lane = lax.broadcasted_iota(jnp.int32, (queries, LANES), 1)
            half = lax.broadcasted_iota(jnp.int32, (queries, LANES), 0) // half_rows
            rope = rope_in[pair].astype(jnp.float32)
            for odd in range(2):
                base = rope_width * (1 - odd)
                mine = (lane < rope_width) if odd == 0 else (lane >= rope_width)
                flag = jnp.where(lane - base == half, 1.0, 0.0)
                q_side[2 * pair + odd] = jnp.where(mine, rope, flag).astype(jnp.bfloat16)

    advance(0)
    for load in loads[:1]:
        load.wait()
    turn_values(0, heads // 2)
    for k in range(1, chunks[0][0] + 1):
        advance(k)
        if k == 1:
            turn_values(heads // 2, heads)
    for load in loads[1:]:
        load.wait()
    side_queries(0, pairs)
    half_at = [half_pos[place["ctx"] * halves + half] for half in range(halves)]
    for half in range(halves):
        q_pos[:, half * half_rows : (half + 1) * half_rows] = half_at[half] * half_rows + lax.broadcasted_iota(
            jnp.int32, (piece_rows, half_rows), 1
        )
    for k in range(chunks[0][1] + 1):
        crossed(k)

    def compute(index, middle):
        _, _, runs = chunks[index]
        first, last = index == 0, index == len(chunks) - 1
        groups = [(piece, slot) for piece, start, count in runs for slot in range(start, start + count)]
        size = len(groups) * piece_rows
        row = 0
        for piece, start, count in runs:
            end = row + count * piece_rows
            block = kv_all[piece, start : start + count].reshape(count * piece_rows, latent_width + rope_width)
            keys[row:end, :] = block[:, :latent_width]
            key_side_even[row:end, :rope_width] = block[:, latent_width:]
            key_side_odd[row:end, rope_width:] = block[:, latent_width:]
            row = end
        flag_lane = lax.broadcasted_iota(jnp.int32, (piece_rows, LANES - rope_width), 1)
        starts = []
        for g, (piece, slot) in enumerate(groups):
            mask = slot_mask(orders[piece], slot, head_size)
            source = sum(
                lax.rem(lax.div(device, bit), 2) * bit if not mask & bit else (1 - lax.rem(lax.div(device, bit), 2)) * bit
                for bit in [1 << b for b in range((slots - 1).bit_length())]
            )
            block = lax.div(source, sources)
            at = half_pos[block]
            flag = jnp.zeros(flag_lane.shape, jnp.float32)
            for half in range(halves):
                flag = jnp.where(flag_lane == half, jnp.where(at <= half_at[half], 0.0, HIDDEN), flag)
            flag = flag.astype(jnp.bfloat16)
            key_side_even[g * piece_rows : (g + 1) * piece_rows, rope_width:] = flag
            key_side_odd[g * piece_rows : (g + 1) * piece_rows, :rope_width] = flag
            starts.append(
                at * half_rows + (source - block * sources) * rows + piece * piece_rows if mask < head_size else None
            )

        blocks = [(b, min(size, b + BLOCK)) for b in range(0, size, BLOCK)]

        def front_tasks(pair, values, scores, slot):
            grown = {}
            tops = [None, None]
            pair_keys = w_uk[pl.ds(2 * pair, 2)].reshape(2 * nope_width, latent_width)
            pair_values = w_uv[pl.ds(2 * pair, 2)].reshape(2 * value_width, latent_width)

            def grow(b):
                begin, end = blocks[b]
                grown[b] = lax.dot_general(
                    keys[begin:end, :], pair_keys, (((1,), (1,)), ((), ())), preferred_element_type=jnp.float32
                ).astype(jnp.bfloat16)

            def value(b):
                begin, end = blocks[b]
                values[:, begin:end] = lax.dot_general(
                    pair_values, keys[begin:end, :], (((1,), (1,)), ((), ())), preferred_element_type=jnp.float32
                ).astype(jnp.bfloat16)

            def score(odd, b):
                begin, end = blocks[b]
                side = (key_side_even, key_side_odd)[odd]
                full = jnp.concatenate(
                    [grown[b][:, odd * nope_width : (odd + 1) * nope_width], side[begin:end, :]], axis=1
                )
                query = jnp.concatenate([q_main[2 * pair + odd], q_side[2 * pair + odd]], axis=1)
                s = lax.dot_general(full, query, (((1,), (1,)), ((), ())), preferred_element_type=jnp.float32)
                base = begin // piece_rows
                g = base
                stop = end // piece_rows
                while g < stop:
                    h = g + 1
                    if starts[g] is None:
                        while h < stop and starts[h] is None:
                            h += 1
                    part = s[(g - base) * piece_rows : (h - base) * piece_rows]
                    if starts[g] is not None:
                        key_pos = starts[g] + lax.broadcasted_iota(jnp.int32, part.shape, 0)
                        part = jnp.where(key_pos <= q_pos[...], part, HIDDEN)
                    scores[odd][g * piece_rows : h * piece_rows, :] = part
                    top = jnp.max(part.reshape(-1, 8, queries), axis=0)
                    tops[odd] = top if tops[odd] is None else jnp.maximum(tops[odd], top)
                    g = h
                if b == len(blocks) - 1:
                    peaks[slot * 2 + odd] = tops[odd]

            tasks = {}
            for b in range(len(blocks)):
                tasks["k", b] = functools.partial(grow, b)
                tasks["v", b] = functools.partial(value, b)
                for odd in range(2):
                    tasks["s", odd, b] = functools.partial(score, odd, b)
            return tasks

        def back_tasks(pair, values, scores, slot):
            state = {}

            def begin_head(odd):
                head = 2 * pair + odd
                top = jnp.broadcast_to(jnp.max(peaks[slot * 2 + odd], axis=0, keepdims=True), (8, queries))
                if not first:
                    before = peak_all[head]
                    top = jnp.maximum(before, top)
                    fade = jnp.exp2((before - top) * scale)
                    state[odd] = [top, fade, den_all[head] * fade, None, None]
                else:
                    state[odd] = [top, None, None, None, None]

            def weigh(odd, b):
                begin, end = blocks[b]
                weight = jnp.exp2((scores[odd][begin:end, :].reshape(-1, 8, queries) - state[odd][0][None]) * scale)
                den = jnp.sum(weight, axis=0)
                state[odd][2] = den if state[odd][2] is None else state[odd][2] + den
                state[odd][4] = weight.reshape(end - begin, queries).astype(jnp.bfloat16)

            def apply(odd, b):
                begin, end = blocks[b]
                part = jnp.dot(
                    values[odd * value_width : (odd + 1) * value_width, begin:end],
                    state[odd][4],
                    preferred_element_type=jnp.float32,
                )
                state[odd][3] = part if state[odd][3] is None else state[odd][3] + part

            def finish(odd):
                head = 2 * pair + odd
                top, fade, den, total, _ = state[odd]
                if not first:
                    total = total + (acc_all[head].reshape(-1, 8, queries) * fade[None]).reshape(total.shape)
                if not last:
                    peak_all[head] = top
                    den_all[head] = den
                    acc_all[head] = total
                else:
                    out = total * (1.0 / jnp.sum(den, axis=0, keepdims=True))
                    out_ref[:, pl.ds(pl.multiple_of(head * value_width, value_width), value_width)] = out.T.astype(
                        out_ref.dtype
                    )

            tasks = {}
            for odd in range(2):
                tasks["b", odd] = functools.partial(begin_head, odd)
                tasks["f", odd] = functools.partial(finish, odd)
                for b in range(len(blocks)):
                    tasks["e", odd, b] = functools.partial(weigh, odd, b)
                    tasks["p", odd, b] = functools.partial(apply, odd, b)
            return tasks

        plan = order_of_tasks(len(blocks), wide)

        def step(front, back, side):
            tasks = {}
            for lane in range(wide):
                if front is not None:
                    here = (side * wide + lane) * 2
                    made = front_tasks(front * wide + lane, values[here // 2], scores[here : here + 2], here // 2)
                    tasks.update({(lane, *name): task for name, task in made.items()})
                if back is not None:
                    here = ((1 - side) * wide + lane) * 2
                    made = back_tasks(back * wide + lane, values[here // 2], scores[here : here + 2], here // 2)
                    tasks.update({(lane, *name): task for name, task in made.items()})
            for name in plan:
                if name in tasks:
                    tasks[name]()

        def steps(begin, end):
            @pl.loop(begin, end)
            def _(turn):
                step(2 * turn + 1, 2 * turn, 1)
                step(2 * turn + 2, 2 * turn + 1, 0)

        count = pairs // wide
        step(0, None, 0)
        turns = count // 2 - 1
        steps(0, turns // 2)
        middle()
        steps(turns // 2, turns)
        step(count - 1, count - 2, 1)
        step(None, count - 1, 0)

    reached = {"own": chunks[0][0], "far": chunks[0][1]}

    def fetch(index):
        while index < len(chunks) and reached["own"] < chunks[index][0]:
            reached["own"] += 1
            advance(reached["own"])

    for index in range(len(chunks)):
        compute(index, lambda: fetch(index + 1))
        while index + 1 < len(chunks) and reached["far"] < chunks[index + 1][1]:
            reached["far"] += 1
            crossed(reached["far"])
    if comm:
        for piece in range(pieces):
            for k in range(hops):
                hop(piece, k).wait_send()
            for k in range(hops + 1):
                across(piece, k).wait_send()


def fused(q_nope, q_rope, kv_latent, half_order, w_uk, w_uv, ctx_size, head_size, comm=True, limit=512, later=1024):
    heads, nope_width, latent_width = w_uk.shape
    value_width = w_uv.shape[2]
    queries = q_nope.shape[0]
    rope_width = q_rope.shape[1] // heads
    rows, width = kv_latent.shape
    pieces = max(1, min(4, rows // 16))
    orders = hop_orders(ctx_size, head_size, pieces)
    hops = len(orders[0])
    piece_rows = rows // pieces
    slots = ctx_size * head_size
    chunks = chunk_plan(hops, pieces, piece_rows, limit, later)
    most = max(sum(count for _, _, count in runs) for _, _, runs in chunks) * piece_rows
    scale = (nope_width + rope_width) ** (-0.5) * math.log2(math.e)
    bf16, f32 = jnp.bfloat16, jnp.float32
    dma = pltpu.SemaphoreType.DMA
    wide = math.gcd(heads // 4, WIDE)
    anywhere = pl.BlockSpec(memory_space=pltpu.HBM)
    return pl.pallas_call(
        functools.partial(fused_kernel, scale, orders, head_size, chunks, comm, wide),
        out_shape=jax.ShapeDtypeStruct((queries, heads * value_width), bf16),
        in_specs=[pl.BlockSpec(memory_space=pltpu.SMEM)] + [anywhere] * 5,
        out_specs=pl.BlockSpec(memory_space=pltpu.VMEM),
        scratch_shapes=[
            pltpu.VMEM((pieces, slots, piece_rows, width), bf16),
            pltpu.VMEM((heads, queries, nope_width), bf16),
            pltpu.VMEM((heads, queries, LANES), bf16),
            pltpu.VMEM((heads // 2, queries, LANES), bf16),
            pltpu.VMEM((heads, nope_width, latent_width), bf16),
            pltpu.VMEM((heads, latent_width, value_width), bf16),
            pltpu.VMEM((heads, value_width, latent_width), bf16),
            pltpu.VMEM((piece_rows, queries), jnp.int32),
            pltpu.VMEM((most, latent_width), bf16),
            pltpu.VMEM((most, LANES), bf16),
            pltpu.VMEM((most, LANES), bf16),
            [pltpu.VMEM((2 * value_width, most), bf16) for _ in range(2 * wide)],
            [pltpu.VMEM((most, queries), f32) for _ in range(4 * wide)],
            pltpu.VMEM((4 * wide, 8, queries), f32),
            pltpu.VMEM((heads, 8, queries), f32),
            pltpu.VMEM((heads, 8, queries), f32),
            pltpu.VMEM((heads, value_width, queries), f32),
            dma((pieces,)),
            dma((2 + heads + heads // 2,)),
            dma((pieces, hops)),
            dma((pieces, hops)),
            dma((pieces, hops + 1)),
            dma((pieces, hops + 1)),
        ],
        compiler_params=pltpu.CompilerParams(
            vmem_limit_bytes=VMEM_MIB * 1024 * 1024,
            **(dict(collective_id=0, has_side_effects=True) if comm else {}),
        ),
        name="attend",
    )(*(pltpu.with_memory_space_constraint(x, pltpu.HBM) for x in (half_order, q_nope, q_rope, kv_latent, w_uk, w_uv)))


def on_device(ctx_size, head_size, q_nope, q_rope, kv_latent, half_order, w_uk, w_uv):
    return fused(q_nope, q_rope, kv_latent, half_order, w_uk, w_uv, ctx_size, head_size)


def solution(mesh):
    return jax.shard_map(
        functools.partial(on_device, mesh.shape["ctx"], mesh.shape["head"]),
        mesh=mesh,
        in_specs=(
            P("ctx", "head"),
            P("ctx", "head"),
            P(("ctx", "head"), None),
            P(),
            P("head", None, None),
            P("head", None, None),
        ),
        out_specs=P("ctx", "head"),
        check_vma=False,
    )
```

```python
import functools
import math

import jax
import jax.numpy as jnp
from jax import lax
from jax.experimental import pallas as pl
from jax.experimental.pallas import tpu as pltpu
from jax.sharding import PartitionSpec as P

LANES = 128
HIDDEN = -1e30


def flipped(index, bit):
    return index + bit * (1 - 2 * ((index // bit) % 2))


def hop_orders(ctx_size, head_size, pieces):
    base = [("ctx", 1 << k) for k in reversed(range(ctx_size.bit_length() - 1))]
    base += [("head", 1 << k) for k in reversed(range(1, head_size.bit_length() - 1))]
    if len(base) < 4:
        return [base] * pieces
    orders = [
        base,
        base[:-2] + [base[-1], base[-2]],
        [base[-2], base[0], base[-1]] + base[1:-2],
        [base[0], base[-1]] + base[1:-2] + [base[-2]],
    ]
    return [orders[piece % 4] for piece in range(pieces)]


def slot_mask(order, slot, head_size):
    hops = order + [("head", 1)]
    taken = [hop for k, hop in enumerate(hops) if (slot >> k) & 1]
    return sum(bit * (head_size if axis == "ctx" else 1) for axis, bit in taken)


def chunk_plan(hops, pieces, piece_rows, limit, later):
    other = 1 << hops
    level = 0
    while level < hops and 2 * pieces * piece_rows << (level + 1) <= limit:
        level += 1
    first = [(piece, side, 1 << level) for side in (0, other) for piece in range(pieces)]
    chunks = [(level, level, first)]
    for k in range(level + 1, hops + 1):
        start, size = 1 << (k - 1), 1 << (k - 1)
        own = [(piece, start, size) for piece in range(pieces)]
        far = [(piece, other + start, size) for piece in range(pieces)]
        side_rows = pieces * size * piece_rows
        if 2 * side_rows <= later:
            chunks.append((k, k, own + far))
            continue
        for side, runs in ((False, own), (True, far)):
            parts = -(-side_rows // later)
            for part in range(parts):
                cut = size // parts
                chunks.append((k, k if side else -1, [(piece, run + part * cut, cut) for piece, run, _ in runs]))
    return chunks


BLOCK = 512
WIDE = 2
VMEM_MIB = 48


def order_of_tasks(blocks, wide):
    every = range(blocks)
    plan = []
    for w in range(wide):
        plan += [(w, "b", 0), (w, "b", 1)]
    for w in range(wide):
        for b in every:
            plan += [(w, "k", b), (w, "e", 0, b), (w, "p", 0, b)]
    for w in range(wide):
        for b in every:
            plan += [(w, "v", b), (w, "e", 1, b), (w, "p", 1, b)]
    for w in range(wide):
        for odd in range(2):
            plan += [(w, "s", odd, b) for b in every]
    for w in range(wide):
        plan += [(w, "f", 0), (w, "f", 1)]
    return plan


def fused_kernel(
    scale,
    orders,
    head_size,
    chunks,
    comm,
    wide,
    half_pos,
    q_nope_hbm,
    q_rope_hbm,
    kv_hbm,
    w_uk_hbm,
    w_uv_hbm,
    out_ref,
    kv_all,
    q_main,
    q_side,
    rope_in,
    w_uk,
    w_uv_in,
    w_uv,
    q_pos,
    key_slots,
    values,
    scores,
    peaks,
    peak_all,
    den_all,
    acc_all,
    own_sem,
    in_sem,
    send_sem,
    recv_sem,
    core_send_sem,
    core_recv_sem,
):
    place = {"ctx": lax.axis_index("ctx"), "head": lax.axis_index("head")}
    device = place["ctx"] * head_size + place["head"]
    pieces, slots, piece_rows, _ = kv_all.shape
    hops = len(orders[0])
    heads, queries, nope_width = q_main.shape
    pairs = heads // 2
    latent_width = w_uk.shape[2]
    value_width = w_uv.shape[1]
    rope_width = kv_all.shape[3] - latent_width
    rows = pieces * piece_rows
    half_rows = rows * slots // half_pos.shape[0]
    halves = queries // half_rows
    sources = half_rows // rows

    def partner(axis, bit):
        return {**place, axis: flipped(place[axis], bit)}

    if comm:
        barrier = pltpu.get_barrier_semaphore()
        greeted = sorted(orders[0]) + [("head", 1)]
        for axis, bit in greeted:
            pl.semaphore_signal(barrier, inc=1, device_id=partner(axis, bit), device_id_type=pl.DeviceIdType.MESH)
    own = []
    for piece in range(pieces):
        own.append(
            pltpu.make_async_copy(
                kv_hbm.at[pl.ds(piece * piece_rows, piece_rows), :], kv_all.at[piece, 0], own_sem.at[piece]
            )
        )
        own[-1].start()
    loads = [
        pltpu.make_async_copy(w_uv_hbm, w_uv_in, in_sem.at[0]),
        pltpu.make_async_copy(w_uk_hbm, w_uk, in_sem.at[1]),
    ]
    for head in range(heads):
        loads.append(
            pltpu.make_async_copy(
                q_nope_hbm.at[:, pl.ds(head * nope_width, nope_width)], q_main.at[head], in_sem.at[2 + head]
            )
        )
    for pair in range(pairs):
        loads.append(
            pltpu.make_async_copy(
                q_rope_hbm.at[:, pl.ds(pair * LANES, LANES)], rope_in.at[pair], in_sem.at[2 + heads + pair]
            )
        )
    for load in loads:
        load.start()

    def hop(piece, k):
        size = 1 << k
        return pltpu.make_async_remote_copy(
            src_ref=kv_all.at[piece, pl.ds(0, size)],
            dst_ref=kv_all.at[piece, pl.ds(size, size)],
            send_sem=send_sem.at[piece, k],
            recv_sem=recv_sem.at[piece, k],
            device_id=partner(*orders[piece][k]),
            device_id_type=pl.DeviceIdType.MESH,
        )

    def across(piece, k):
        start, size = (0, 1) if k == 0 else (1 << (k - 1), 1 << (k - 1))
        return pltpu.make_async_remote_copy(
            src_ref=kv_all.at[piece, pl.ds(start, size)],
            dst_ref=kv_all.at[piece, pl.ds(slots // 2 + start, size)],
            send_sem=core_send_sem.at[piece, k],
            recv_sem=core_recv_sem.at[piece, k],
            device_id=partner("head", 1),
            device_id_type=pl.DeviceIdType.MESH,
        )

    def advance(k):
        for piece in range(pieces):
            if k == 0:
                own[piece].wait()
            elif comm:
                hop(piece, k - 1).wait_recv()
            if comm:
                if k < hops:
                    hop(piece, k).start()
                across(piece, k).start()

    def crossed(k):
        if comm:
            for piece in range(pieces):
                across(piece, k).wait_recv()

    if comm:
        pl.semaphore_wait(barrier, len(greeted))

    def turn_values(first, last):
        @pl.loop(first, last)
        def _(head):
            w_uv[head] = w_uv_in[head].T

    def side_queries(first, last):
        @pl.loop(first, last)
        def _(pair):
            lane = lax.broadcasted_iota(jnp.int32, (queries, LANES), 1)
            half = lax.broadcasted_iota(jnp.int32, (queries, LANES), 0) // half_rows
            rope = rope_in[pair].astype(jnp.float32)
            for odd in range(2):
                base = rope_width * (1 - odd)
                mine = (lane < rope_width) if odd == 0 else (lane >= rope_width)
                flag = jnp.where(lane - base == half, 1.0, 0.0)
                q_side[2 * pair + odd] = jnp.where(mine, rope, flag).astype(jnp.bfloat16)

    def prepare_operands(part, parts):
        if part == 0:
            loads[0].wait()
        turn_values(heads * part // parts, heads * (part + 1) // parts)
        if part == parts - 1:
            for load in loads[1:]:
                load.wait()
            side_queries(0, pairs)

    parts = max(1, chunks[0][0])
    advance(0)
    for part in range(parts):
        prepare_operands(part, parts)
        if part < chunks[0][0]:
            advance(part + 1)
    half_at = [half_pos[place["ctx"] * halves + half] for half in range(halves)]
    for half in range(halves):
        q_pos[:, half * half_rows : (half + 1) * half_rows] = half_at[half] * half_rows + lax.broadcasted_iota(
            jnp.int32, (piece_rows, half_rows), 1
        )
    for k in range(chunks[0][1] + 1):
        crossed(k)

    def blocks_of(size):
        return [(b, min(size, b + BLOCK)) for b in range(0, size, BLOCK)]

    def prepare(index):
        _, _, runs = chunks[index]
        keys, key_side_even, key_side_odd = key_slots[index % 2]
        first, last = index == 0, index == len(chunks) - 1
        groups = [(piece, slot) for piece, start, count in runs for slot in range(start, start + count)]
        size = len(groups) * piece_rows
        row = 0
        for piece, start, count in runs:
            end = row + count * piece_rows
            block = kv_all[piece, start : start + count].reshape(count * piece_rows, latent_width + rope_width)
            keys[row:end, :] = block[:, :latent_width]
            key_side_even[row:end, :rope_width] = block[:, latent_width:]
            key_side_odd[row:end, rope_width:] = block[:, latent_width:]
            row = end
        flag_lane = lax.broadcasted_iota(jnp.int32, (piece_rows, LANES - rope_width), 1)
        starts = []
        for g, (piece, slot) in enumerate(groups):
            mask = slot_mask(orders[piece], slot, head_size)
            source = sum(
                lax.rem(lax.div(device, bit), 2) * bit if not mask & bit else (1 - lax.rem(lax.div(device, bit), 2)) * bit
                for bit in [1 << b for b in range((slots - 1).bit_length())]
            )
            block = lax.div(source, sources)
            at = half_pos[block]
            flag = jnp.zeros(flag_lane.shape, jnp.float32)
            for half in range(halves):
                flag = jnp.where(flag_lane == half, jnp.where(at <= half_at[half], 0.0, HIDDEN), flag)
            flag = flag.astype(jnp.bfloat16)
            key_side_even[g * piece_rows : (g + 1) * piece_rows, rope_width:] = flag
            key_side_odd[g * piece_rows : (g + 1) * piece_rows, :rope_width] = flag
            starts.append(
                at * half_rows + (source - block * sources) * rows + piece * piece_rows if mask < head_size else None
            )

        return first, last, groups, size, starts, (keys, key_side_even, key_side_odd)

    def front_tasks(chunk, pair, values, scores, slot):
        _, _, groups, size, starts, (keys, key_side_even, key_side_odd) = chunk
        blocks = blocks_of(size)
        grown = {}
        tops = [None, None]
        pair_keys = w_uk[pl.ds(2 * pair, 2)].reshape(2 * nope_width, latent_width)
        pair_values = w_uv[pl.ds(2 * pair, 2)].reshape(2 * value_width, latent_width)

        def grow(b):
            begin, end = blocks[b]
            grown[b] = lax.dot_general(
                keys[begin:end, :], pair_keys, (((1,), (1,)), ((), ())), preferred_element_type=jnp.float32
            ).astype(jnp.bfloat16)

        def value(b):
            begin, end = blocks[b]
            values[:, begin:end] = lax.dot_general(
                pair_values, keys[begin:end, :], (((1,), (1,)), ((), ())), preferred_element_type=jnp.float32
            ).astype(jnp.bfloat16)

        def score(odd, b):
            begin, end = blocks[b]
            side = (key_side_even, key_side_odd)[odd]
            full = jnp.concatenate(
                [grown[b][:, odd * nope_width : (odd + 1) * nope_width], side[begin:end, :]], axis=1
            )
            query = jnp.concatenate([q_main[2 * pair + odd], q_side[2 * pair + odd]], axis=1)
            s = lax.dot_general(full, query, (((1,), (1,)), ((), ())), preferred_element_type=jnp.float32)
            base = begin // piece_rows
            g = base
            stop = end // piece_rows
            while g < stop:
                h = g + 1
                if starts[g] is None:
                    while h < stop and starts[h] is None:
                        h += 1
                part = s[(g - base) * piece_rows : (h - base) * piece_rows]
                if starts[g] is not None:
                    key_pos = starts[g] + lax.broadcasted_iota(jnp.int32, part.shape, 0)
                    part = jnp.where(key_pos <= q_pos[...], part, HIDDEN)
                scores[odd][g * piece_rows : h * piece_rows, :] = part
                top = jnp.max(part.reshape(-1, 8, queries), axis=0)
                tops[odd] = top if tops[odd] is None else jnp.maximum(tops[odd], top)
                g = h
            if b == len(blocks) - 1:
                peaks[slot * 2 + odd] = tops[odd]

        tasks = {}
        for b in range(len(blocks)):
            tasks["k", b] = functools.partial(grow, b)
            tasks["v", b] = functools.partial(value, b)
            for odd in range(2):
                tasks["s", odd, b] = functools.partial(score, odd, b)
        return tasks

    def back_tasks(chunk, pair, values, scores, slot):
        first, last, _, size, _, _ = chunk
        blocks = blocks_of(size)
        state = {}

        def begin_head(odd):
            head = 2 * pair + odd
            top = jnp.broadcast_to(jnp.max(peaks[slot * 2 + odd], axis=0, keepdims=True), (8, queries))
            if not first:
                before = peak_all[head]
                top = jnp.maximum(before, top)
                fade = jnp.exp2((before - top) * scale)
                state[odd] = [top, fade, den_all[head] * fade, None, None]
            else:
                state[odd] = [top, None, None, None, None]

        def weigh(odd, b):
            begin, end = blocks[b]
            weight = jnp.exp2((scores[odd][begin:end, :].reshape(-1, 8, queries) - state[odd][0][None]) * scale)
            den = jnp.sum(weight, axis=0)
            state[odd][2] = den if state[odd][2] is None else state[odd][2] + den
            state[odd][4] = weight.reshape(end - begin, queries).astype(jnp.bfloat16)

        def apply(odd, b):
            begin, end = blocks[b]
            part = jnp.dot(
                values[odd * value_width : (odd + 1) * value_width, begin:end],
                state[odd][4],
                preferred_element_type=jnp.float32,
            )
            state[odd][3] = part if state[odd][3] is None else state[odd][3] + part

        def finish(odd):
            head = 2 * pair + odd
            top, fade, den, total, _ = state[odd]
            if not first:
                total = total + (acc_all[head].reshape(-1, 8, queries) * fade[None]).reshape(total.shape)
            if not last:
                peak_all[head] = top
                den_all[head] = den
                acc_all[head] = total
            else:
                out = total * (1.0 / jnp.sum(den, axis=0, keepdims=True))
                out_ref[:, pl.ds(pl.multiple_of(head * value_width, value_width), value_width)] = out.T.astype(
                    out_ref.dtype
                )

        tasks = {}
        for odd in range(2):
            tasks["b", odd] = functools.partial(begin_head, odd)
            tasks["f", odd] = functools.partial(finish, odd)
            for b in range(len(blocks)):
                tasks["e", odd, b] = functools.partial(weigh, odd, b)
                tasks["p", odd, b] = functools.partial(apply, odd, b)
        return tasks

    def step(front, back, side):
        tasks = {}
        most = 0
        for lane in range(wide):
            if front is not None:
                chunk, at = front
                here = (side * wide + lane) * 2
                made = front_tasks(chunk, at * wide + lane, values[here // 2], scores[here : here + 2], here // 2)
                tasks.update({(lane, *name): task for name, task in made.items()})
                most = max(most, len(blocks_of(chunk[3])))
            if back is not None:
                chunk, at = back
                here = ((1 - side) * wide + lane) * 2
                made = back_tasks(chunk, at * wide + lane, values[here // 2], scores[here : here + 2], here // 2)
                tasks.update({(lane, *name): task for name, task in made.items()})
                most = max(most, len(blocks_of(chunk[3])))
        for name in order_of_tasks(most, wide):
            if name in tasks:
                tasks[name]()

    def steps(chunk, begin, end):
        @pl.loop(begin, end)
        def _(turn):
            step((chunk, 2 * turn + 1), (chunk, 2 * turn), 1)
            step((chunk, 2 * turn + 2), (chunk, 2 * turn + 1), 0)

    reached = {"own": chunks[0][0], "far": chunks[0][1]}

    def fetch(index):
        while index < len(chunks) and reached["own"] < chunks[index][0]:
            reached["own"] += 1
            advance(reached["own"])

    count = pairs // wide
    turns = count // 2 - 1
    chunk = prepare(0)
    step((chunk, 0), None, 0)
    for index in range(len(chunks)):
        cut = -(-2 * turns // 3)
        steps(chunk, 0, cut)
        fetch(index + 1)
        steps(chunk, cut, turns)
        step((chunk, count - 1), (chunk, count - 2), 1)
        if index + 1 == len(chunks):
            step(None, (chunk, count - 1), 0)
            break
        while reached["far"] < chunks[index + 1][1]:
            reached["far"] += 1
            crossed(reached["far"])
        following = prepare(index + 1)
        step((following, 0), (chunk, count - 1), 0)
        chunk = following
    if comm:
        for piece in range(pieces):
            for k in range(hops):
                hop(piece, k).wait_send()
            for k in range(hops + 1):
                across(piece, k).wait_send()


def fused(q_nope, q_rope, kv_latent, half_order, w_uk, w_uv, ctx_size, head_size, comm=True, limit=256, later=1024):
    heads, nope_width, latent_width = w_uk.shape
    value_width = w_uv.shape[2]
    queries = q_nope.shape[0]
    rope_width = q_rope.shape[1] // heads
    rows, width = kv_latent.shape
    pieces = max(1, min(4, rows // 16))
    orders = hop_orders(ctx_size, head_size, pieces)
    hops = len(orders[0])
    piece_rows = rows // pieces
    slots = ctx_size * head_size
    chunks = chunk_plan(hops, pieces, piece_rows, limit, later)
    most = max(sum(count for _, _, count in runs) for _, _, runs in chunks) * piece_rows
    scale = (nope_width + rope_width) ** (-0.5) * math.log2(math.e)
    bf16, f32 = jnp.bfloat16, jnp.float32
    dma = pltpu.SemaphoreType.DMA
    wide = math.gcd(heads // 4, WIDE)
    anywhere = pl.BlockSpec(memory_space=pltpu.HBM)
    return pl.pallas_call(
        functools.partial(fused_kernel, scale, orders, head_size, chunks, comm, wide),
        out_shape=jax.ShapeDtypeStruct((queries, heads * value_width), bf16),
        in_specs=[pl.BlockSpec(memory_space=pltpu.SMEM)] + [anywhere] * 5,
        out_specs=pl.BlockSpec(memory_space=pltpu.VMEM),
        scratch_shapes=[
            pltpu.VMEM((pieces, slots, piece_rows, width), bf16),
            pltpu.VMEM((heads, queries, nope_width), bf16),
            pltpu.VMEM((heads, queries, LANES), bf16),
            pltpu.VMEM((heads // 2, queries, LANES), bf16),
            pltpu.VMEM((heads, nope_width, latent_width), bf16),
            pltpu.VMEM((heads, latent_width, value_width), bf16),
            pltpu.VMEM((heads, value_width, latent_width), bf16),
            pltpu.VMEM((piece_rows, queries), jnp.int32),
            [
                (pltpu.VMEM((size, latent_width), bf16), pltpu.VMEM((size, LANES), bf16), pltpu.VMEM((size, LANES), bf16))
                for size in (most, most)
            ],
            [pltpu.VMEM((2 * value_width, most), bf16) for _ in range(2 * wide)],
            [pltpu.VMEM((most, queries), f32) for _ in range(4 * wide)],
            pltpu.VMEM((4 * wide, 8, queries), f32),
            pltpu.VMEM((heads, 8, queries), f32),
            pltpu.VMEM((heads, 8, queries), f32),
            pltpu.VMEM((heads, value_width, queries), f32),
            dma((pieces,)),
            dma((2 + heads + heads // 2,)),
            dma((pieces, hops)),
            dma((pieces, hops)),
            dma((pieces, hops + 1)),
            dma((pieces, hops + 1)),
        ],
        compiler_params=pltpu.CompilerParams(
            vmem_limit_bytes=VMEM_MIB * 1024 * 1024,
            **(dict(collective_id=0, has_side_effects=True) if comm else {}),
        ),
        name="attend",
    )(*(pltpu.with_memory_space_constraint(x, pltpu.HBM) for x in (half_order, q_nope, q_rope, kv_latent, w_uk, w_uv)))


def on_device(ctx_size, head_size, q_nope, q_rope, kv_latent, half_order, w_uk, w_uv):
    return fused(q_nope, q_rope, kv_latent, half_order, w_uk, w_uv, ctx_size, head_size)


def solution(mesh):
    return jax.shard_map(
        functools.partial(on_device, mesh.shape["ctx"], mesh.shape["head"]),
        mesh=mesh,
        in_specs=(
            P("ctx", "head"),
            P("ctx", "head"),
            P(("ctx", "head"), None),
            P(),
            P("head", None, None),
            P("head", None, None),
        ),
        out_specs=P("ctx", "head"),
        check_vma=False,
    )
```

```python
import functools
import math

import jax
import jax.numpy as jnp
from jax import lax
from jax.experimental import pallas as pl
from jax.experimental.pallas import tpu as pltpu
from jax.sharding import PartitionSpec as P

LANES = 128
HIDDEN = -1e30


def flipped(index, bit):
    return index + bit * (1 - 2 * ((index // bit) % 2))


def hop_orders(ctx_size, head_size, pieces):
    base = [("ctx", 1 << k) for k in reversed(range(ctx_size.bit_length() - 1))]
    base += [("head", 1 << k) for k in reversed(range(1, head_size.bit_length() - 1))]
    if len(base) < 4:
        return [base] * pieces
    orders = [
        base,
        base[:-2] + [base[-1], base[-2]],
        [base[-2], base[0], base[-1]] + base[1:-2],
        [base[0], base[-1]] + base[1:-2] + [base[-2]],
    ]
    return [orders[piece % 4] for piece in range(pieces)]


def slot_mask(order, slot, head_size):
    hops = order + [("head", 1)]
    taken = [hop for k, hop in enumerate(hops) if (slot >> k) & 1]
    return sum(bit * (head_size if axis == "ctx" else 1) for axis, bit in taken)


def chunk_plan(hops, pieces, piece_rows, limit, later):
    other = 1 << hops
    level = 0
    while level < hops and 2 * pieces * piece_rows << (level + 1) <= limit:
        level += 1
    first = [(piece, side, 1 << level) for side in (0, other) for piece in range(pieces)]
    chunks = [(level, level, first)]
    for k in range(level + 1, hops + 1):
        start, size = 1 << (k - 1), 1 << (k - 1)
        own = [(piece, start, size) for piece in range(pieces)]
        far = [(piece, other + start, size) for piece in range(pieces)]
        side_rows = pieces * size * piece_rows
        if 2 * side_rows <= later:
            chunks.append((k, k, own + far))
            continue
        for side, runs in ((False, own), (True, far)):
            parts = -(-side_rows // later)
            for part in range(parts):
                cut = size // parts
                chunks.append((k, k if side else -1, [(piece, run + part * cut, cut) for piece, run, _ in runs]))
    return chunks


BLOCK = 512
WIDE = 2
VMEM_MIB = 48


def order_of_tasks(blocks, wide):
    every = range(blocks)
    plan = []
    for w in range(wide):
        plan += [(w, "b", 0), (w, "b", 1)]
    for w in range(wide):
        for b in every:
            plan += [(w, "k", b), (w, "e", 0, b), (w, "p", 0, b)]
    for w in range(wide):
        for b in every:
            plan += [(w, "v", b), (w, "e", 1, b), (w, "p", 1, b)]
    for w in range(wide):
        for odd in range(2):
            plan += [(w, "s", odd, b) for b in every]
    for w in range(wide):
        plan += [(w, "f", 0), (w, "f", 1)]
    return plan


def fused_kernel(
    scale,
    orders,
    head_size,
    chunks,
    comm,
    wide,
    half_pos,
    q_nope_hbm,
    q_rope_hbm,
    kv_hbm,
    w_uk_hbm,
    w_uv_hbm,
    out_ref,
    kv_all,
    q_main,
    q_side,
    rope_in,
    w_uk,
    w_uv_in,
    w_uv,
    q_pos,
    key_slots,
    values,
    scores,
    peaks,
    peak_all,
    den_all,
    acc_all,
    own_sem,
    in_sem,
    send_sem,
    recv_sem,
    core_send_sem,
    core_recv_sem,
):
    place = {"ctx": lax.axis_index("ctx"), "head": lax.axis_index("head")}
    device = place["ctx"] * head_size + place["head"]
    pieces, slots, piece_rows, _ = kv_all.shape
    hops = len(orders[0])
    heads, queries, nope_width = q_main.shape
    pairs = heads // 2
    latent_width = w_uk.shape[2]
    value_width = w_uv.shape[1]
    rope_width = kv_all.shape[3] - latent_width
    rows = pieces * piece_rows
    half_rows = rows * slots // half_pos.shape[0]
    halves = queries // half_rows
    sources = half_rows // rows

    def partner(axis, bit):
        return {**place, axis: flipped(place[axis], bit)}

    if comm:
        barrier = pltpu.get_barrier_semaphore()
        greeted = sorted(orders[0]) + [("head", 1)]
        for axis, bit in greeted:
            pl.semaphore_signal(barrier, inc=1, device_id=partner(axis, bit), device_id_type=pl.DeviceIdType.MESH)
    own = []
    for piece in range(pieces):
        own.append(
            pltpu.make_async_copy(
                kv_hbm.at[pl.ds(piece * piece_rows, piece_rows), :], kv_all.at[piece, 0], own_sem.at[piece]
            )
        )
        own[-1].start()
    loads = [
        pltpu.make_async_copy(w_uv_hbm, w_uv_in, in_sem.at[0]),
        pltpu.make_async_copy(w_uk_hbm, w_uk, in_sem.at[1]),
    ]
    for head in range(heads):
        loads.append(
            pltpu.make_async_copy(
                q_nope_hbm.at[:, pl.ds(head * nope_width, nope_width)], q_main.at[head], in_sem.at[2 + head]
            )
        )
    for pair in range(pairs):
        loads.append(
            pltpu.make_async_copy(
                q_rope_hbm.at[:, pl.ds(pair * LANES, LANES)], rope_in.at[pair], in_sem.at[2 + heads + pair]
            )
        )
    for load in loads:
        load.start()

    def hop(piece, k):
        size = 1 << k
        return pltpu.make_async_remote_copy(
            src_ref=kv_all.at[piece, pl.ds(0, size)],
            dst_ref=kv_all.at[piece, pl.ds(size, size)],
            send_sem=send_sem.at[piece, k],
            recv_sem=recv_sem.at[piece, k],
            device_id=partner(*orders[piece][k]),
            device_id_type=pl.DeviceIdType.MESH,
        )

    def across(piece, k):
        start, size = (0, 1) if k == 0 else (1 << (k - 1), 1 << (k - 1))
        return pltpu.make_async_remote_copy(
            src_ref=kv_all.at[piece, pl.ds(start, size)],
            dst_ref=kv_all.at[piece, pl.ds(slots // 2 + start, size)],
            send_sem=core_send_sem.at[piece, k],
            recv_sem=core_recv_sem.at[piece, k],
            device_id=partner("head", 1),
            device_id_type=pl.DeviceIdType.MESH,
        )

    def advance(k):
        for piece in range(pieces):
            if k == 0:
                own[piece].wait()
            elif comm:
                hop(piece, k - 1).wait_recv()
            if comm:
                if k < hops:
                    hop(piece, k).start()
                across(piece, k).start()

    def crossed(k):
        if comm:
            for piece in range(pieces):
                across(piece, k).wait_recv()

    if comm:
        pl.semaphore_wait(barrier, len(greeted))

    def turn_values(first, last):
        @pl.loop(first, last)
        def _(head):
            w_uv[head] = w_uv_in[head].T

    def side_queries(first, last):
        @pl.loop(first, last)
        def _(pair):
            lane = lax.broadcasted_iota(jnp.int32, (queries, LANES), 1)
            half = lax.broadcasted_iota(jnp.int32, (queries, LANES), 0) // half_rows
            rope = rope_in[pair].astype(jnp.float32)
            for odd in range(2):
                base = rope_width * (1 - odd)
                mine = (lane < rope_width) if odd == 0 else (lane >= rope_width)
                flag = jnp.where(lane - base == half, 1.0, 0.0)
                q_side[2 * pair + odd] = jnp.where(mine, rope, flag).astype(jnp.bfloat16)

    def prepare_operands(part, parts):
        if part == 0:
            loads[0].wait()
        turn_values(heads * part // parts, heads * (part + 1) // parts)
        if part == parts - 1:
            for load in loads[1:]:
                load.wait()
            side_queries(0, pairs)

    parts = max(1, chunks[0][0])
    advance(0)
    for part in range(parts):
        prepare_operands(part, parts)
        if part < chunks[0][0]:
            advance(part + 1)
    half_at = [half_pos[place["ctx"] * halves + half] for half in range(halves)]
    for half in range(halves):
        q_pos[:, half * half_rows : (half + 1) * half_rows] = half_at[half] * half_rows + lax.broadcasted_iota(
            jnp.int32, (piece_rows, half_rows), 1
        )
    for k in range(chunks[0][1] + 1):
        crossed(k)

    def blocks_of(size):
        return [(b, min(size, b + BLOCK)) for b in range(0, size, BLOCK)]

    def prepare(index):
        _, _, runs = chunks[index]
        keys, key_side_even, key_side_odd = key_slots[index % 2]
        first, last = index == 0, index == len(chunks) - 1
        groups = [(piece, slot) for piece, start, count in runs for slot in range(start, start + count)]
        size = len(groups) * piece_rows
        row = 0
        for piece, start, count in runs:
            end = row + count * piece_rows
            block = kv_all[piece, start : start + count].reshape(count * piece_rows, latent_width + rope_width)
            keys[row:end, :] = block[:, :latent_width]
            key_side_even[row:end, :rope_width] = block[:, latent_width:]
            key_side_odd[row:end, rope_width:] = block[:, latent_width:]
            row = end
        flag_lane = lax.broadcasted_iota(jnp.int32, (piece_rows, LANES - rope_width), 1)
        starts = []
        for g, (piece, slot) in enumerate(groups):
            mask = slot_mask(orders[piece], slot, head_size)
            source = sum(
                lax.rem(lax.div(device, bit), 2) * bit if not mask & bit else (1 - lax.rem(lax.div(device, bit), 2)) * bit
                for bit in [1 << b for b in range((slots - 1).bit_length())]
            )
            block = lax.div(source, sources)
            at = half_pos[block]
            flag = jnp.zeros(flag_lane.shape, jnp.float32)
            for half in range(halves):
                flag = jnp.where(flag_lane == half, jnp.where(at <= half_at[half], 0.0, HIDDEN), flag)
            flag = flag.astype(jnp.bfloat16)
            key_side_even[g * piece_rows : (g + 1) * piece_rows, rope_width:] = flag
            key_side_odd[g * piece_rows : (g + 1) * piece_rows, :rope_width] = flag
            starts.append(
                at * half_rows + (source - block * sources) * rows + piece * piece_rows if mask < head_size else None
            )

        return first, last, groups, size, starts, (keys, key_side_even, key_side_odd)

    def front_tasks(chunk, pair, values, scores, slot):
        _, _, groups, size, starts, (keys, key_side_even, key_side_odd) = chunk
        blocks = blocks_of(size)
        grown = {}
        tops = [None, None]
        pair_keys = w_uk[pl.ds(2 * pair, 2)].reshape(2 * nope_width, latent_width)
        pair_values = w_uv[pl.ds(2 * pair, 2)].reshape(2 * value_width, latent_width)

        def grow(b):
            begin, end = blocks[b]
            grown[b] = lax.dot_general(
                keys[begin:end, :], pair_keys, (((1,), (1,)), ((), ())), preferred_element_type=jnp.float32
            ).astype(jnp.bfloat16)

        def value(b):
            begin, end = blocks[b]
            values[:, begin:end] = lax.dot_general(
                pair_values, keys[begin:end, :], (((1,), (1,)), ((), ())), preferred_element_type=jnp.float32
            ).astype(jnp.bfloat16)

        def score(odd, b):
            begin, end = blocks[b]
            side = (key_side_even, key_side_odd)[odd]
            full = jnp.concatenate(
                [grown[b][:, odd * nope_width : (odd + 1) * nope_width], side[begin:end, :]], axis=1
            )
            query = jnp.concatenate([q_main[2 * pair + odd], q_side[2 * pair + odd]], axis=1)
            s = lax.dot_general(full, query, (((1,), (1,)), ((), ())), preferred_element_type=jnp.float32)
            base = begin // piece_rows
            g = base
            stop = end // piece_rows
            while g < stop:
                h = g + 1
                if starts[g] is None:
                    while h < stop and starts[h] is None:
                        h += 1
                part = s[(g - base) * piece_rows : (h - base) * piece_rows]
                if starts[g] is not None:
                    key_pos = starts[g] + lax.broadcasted_iota(jnp.int32, part.shape, 0)
                    part = jnp.where(key_pos <= q_pos[...], part, HIDDEN)
                scores[odd][g * piece_rows : h * piece_rows, :] = part
                top = jnp.max(part.reshape(-1, 8, queries), axis=0)
                tops[odd] = top if tops[odd] is None else jnp.maximum(tops[odd], top)
                g = h
            if b == len(blocks) - 1:
                peaks[slot * 2 + odd] = tops[odd]

        tasks = {}
        for b in range(len(blocks)):
            tasks["k", b] = functools.partial(grow, b)
            tasks["v", b] = functools.partial(value, b)
            for odd in range(2):
                tasks["s", odd, b] = functools.partial(score, odd, b)
        return tasks

    def back_tasks(chunk, pair, values, scores, slot):
        first, last, _, size, _, _ = chunk
        blocks = blocks_of(size)
        state = {}

        def begin_head(odd):
            head = 2 * pair + odd
            top = jnp.broadcast_to(jnp.max(peaks[slot * 2 + odd], axis=0, keepdims=True), (8, queries))
            if not first:
                before = peak_all[head]
                top = jnp.maximum(before, top)
                fade = jnp.exp2((before - top) * scale)
                state[odd] = [top, fade, den_all[head] * fade, None, None]
            else:
                state[odd] = [top, None, None, None, None]

        def weigh(odd, b):
            begin, end = blocks[b]
            weight = jnp.exp2((scores[odd][begin:end, :].reshape(-1, 8, queries) - state[odd][0][None]) * scale)
            den = jnp.sum(weight, axis=0)
            state[odd][2] = den if state[odd][2] is None else state[odd][2] + den
            state[odd][4] = weight.reshape(end - begin, queries).astype(jnp.bfloat16)

        def apply(odd, b):
            begin, end = blocks[b]
            part = jnp.dot(
                values[odd * value_width : (odd + 1) * value_width, begin:end],
                state[odd][4],
                preferred_element_type=jnp.float32,
            )
            state[odd][3] = part if state[odd][3] is None else state[odd][3] + part

        def finish(odd):
            head = 2 * pair + odd
            top, fade, den, total, _ = state[odd]
            if not first:
                total = total + (acc_all[head].reshape(-1, 8, queries) * fade[None]).reshape(total.shape)
            if not last:
                peak_all[head] = top
                den_all[head] = den
                acc_all[head] = total
            else:
                out = total * (1.0 / jnp.sum(den, axis=0, keepdims=True))
                out_ref[:, pl.ds(pl.multiple_of(head * value_width, value_width), value_width)] = out.T.astype(
                    out_ref.dtype
                )

        tasks = {}
        for odd in range(2):
            tasks["b", odd] = functools.partial(begin_head, odd)
            tasks["f", odd] = functools.partial(finish, odd)
            for b in range(len(blocks)):
                tasks["e", odd, b] = functools.partial(weigh, odd, b)
                tasks["p", odd, b] = functools.partial(apply, odd, b)
        return tasks

    def step(front, back, side):
        tasks = {}
        most = 0
        for lane in range(wide):
            if front is not None:
                chunk, at = front
                here = (side * wide + lane) * 2
                made = front_tasks(chunk, at * wide + lane, values[here // 2], scores[here : here + 2], here // 2)
                tasks.update({(lane, *name): task for name, task in made.items()})
                most = max(most, len(blocks_of(chunk[3])))
            if back is not None:
                chunk, at = back
                here = ((1 - side) * wide + lane) * 2
                made = back_tasks(chunk, at * wide + lane, values[here // 2], scores[here : here + 2], here // 2)
                tasks.update({(lane, *name): task for name, task in made.items()})
                most = max(most, len(blocks_of(chunk[3])))
        for name in order_of_tasks(most, wide):
            if name in tasks:
                tasks[name]()

    def steps(chunk, begin, end):
        @pl.loop(begin, end)
        def _(turn):
            step((chunk, 2 * turn + 1), (chunk, 2 * turn), 1)
            step((chunk, 2 * turn + 2), (chunk, 2 * turn + 1), 0)

    reached = {"own": chunks[0][0], "far": chunks[0][1]}

    def fetch(index):
        while index < len(chunks) and reached["own"] < chunks[index][0]:
            reached["own"] += 1
            advance(reached["own"])

    count = pairs // wide
    turns = count // 2 - 1
    chunk = prepare(0)
    step((chunk, 0), None, 0)
    for index in range(len(chunks)):
        cut = turns if index + 2 == len(chunks) else -(-2 * turns // 3)
        steps(chunk, 0, cut)
        fetch(index + 1)
        steps(chunk, cut, turns)
        step((chunk, count - 1), (chunk, count - 2), 1)
        if index + 1 == len(chunks):
            step(None, (chunk, count - 1), 0)
            break
        while reached["far"] < chunks[index + 1][1]:
            reached["far"] += 1
            crossed(reached["far"])
        following = prepare(index + 1)
        step((following, 0), (chunk, count - 1), 0)
        chunk = following
    if comm:
        for piece in range(pieces):
            for k in range(hops):
                hop(piece, k).wait_send()
            for k in range(hops + 1):
                across(piece, k).wait_send()


def fused(q_nope, q_rope, kv_latent, half_order, w_uk, w_uv, ctx_size, head_size, comm=True, limit=256, later=1024):
    heads, nope_width, latent_width = w_uk.shape
    value_width = w_uv.shape[2]
    queries = q_nope.shape[0]
    rope_width = q_rope.shape[1] // heads
    rows, width = kv_latent.shape
    pieces = max(1, min(4, rows // 16))
    orders = hop_orders(ctx_size, head_size, pieces)
    hops = len(orders[0])
    piece_rows = rows // pieces
    slots = ctx_size * head_size
    chunks = chunk_plan(hops, pieces, piece_rows, limit, later)
    most = max(sum(count for _, _, count in runs) for _, _, runs in chunks) * piece_rows
    scale = (nope_width + rope_width) ** (-0.5) * math.log2(math.e)
    bf16, f32 = jnp.bfloat16, jnp.float32
    dma = pltpu.SemaphoreType.DMA
    wide = math.gcd(heads // 4, WIDE)
    anywhere = pl.BlockSpec(memory_space=pltpu.HBM)
    return pl.pallas_call(
        functools.partial(fused_kernel, scale, orders, head_size, chunks, comm, wide),
        out_shape=jax.ShapeDtypeStruct((queries, heads * value_width), bf16),
        in_specs=[pl.BlockSpec(memory_space=pltpu.SMEM)] + [anywhere] * 5,
        out_specs=pl.BlockSpec(memory_space=pltpu.VMEM),
        scratch_shapes=[
            pltpu.VMEM((pieces, slots, piece_rows, width), bf16),
            pltpu.VMEM((heads, queries, nope_width), bf16),
            pltpu.VMEM((heads, queries, LANES), bf16),
            pltpu.VMEM((heads // 2, queries, LANES), bf16),
            pltpu.VMEM((heads, nope_width, latent_width), bf16),
            pltpu.VMEM((heads, latent_width, value_width), bf16),
            pltpu.VMEM((heads, value_width, latent_width), bf16),
            pltpu.VMEM((piece_rows, queries), jnp.int32),
            [
                (pltpu.VMEM((size, latent_width), bf16), pltpu.VMEM((size, LANES), bf16), pltpu.VMEM((size, LANES), bf16))
                for size in (most, most)
            ],
            [pltpu.VMEM((2 * value_width, most), bf16) for _ in range(2 * wide)],
            [pltpu.VMEM((most, queries), f32) for _ in range(4 * wide)],
            pltpu.VMEM((4 * wide, 8, queries), f32),
            pltpu.VMEM((heads, 8, queries), f32),
            pltpu.VMEM((heads, 8, queries), f32),
            pltpu.VMEM((heads, value_width, queries), f32),
            dma((pieces,)),
            dma((2 + heads + heads // 2,)),
            dma((pieces, hops)),
            dma((pieces, hops)),
            dma((pieces, hops + 1)),
            dma((pieces, hops + 1)),
        ],
        compiler_params=pltpu.CompilerParams(
            vmem_limit_bytes=VMEM_MIB * 1024 * 1024,
            **(dict(collective_id=0, has_side_effects=True) if comm else {}),
        ),
        name="attend",
    )(*(pltpu.with_memory_space_constraint(x, pltpu.HBM) for x in (half_order, q_nope, q_rope, kv_latent, w_uk, w_uv)))


def on_device(ctx_size, head_size, q_nope, q_rope, kv_latent, half_order, w_uk, w_uv):
    return fused(q_nope, q_rope, kv_latent, half_order, w_uk, w_uv, ctx_size, head_size)


def solution(mesh):
    return jax.shard_map(
        functools.partial(on_device, mesh.shape["ctx"], mesh.shape["head"]),
        mesh=mesh,
        in_specs=(
            P("ctx", "head"),
            P("ctx", "head"),
            P(("ctx", "head"), None),
            P(),
            P("head", None, None),
            P("head", None, None),
        ),
        out_specs=P("ctx", "head"),
        check_vma=False,
    )
```
